32 devices in a mesh: leaf: 8 (over z, x), sub: 4 (over y, core).
Axes of the slice: x: 2, y: 2, z: 4, core: 2. Of those that a mesh axis runs over, the one named last changes fastest.
Arguments:
- points: float32 [65536, 64], P(('leaf', 'sub')), may hold values from -6 to 6
- leaf_maps: float32 [128, 128, 512], P(('leaf', 'sub')), may hold values from -0.25 to 0.25
- root_maps: float32 [128, 128, 512], P(('leaf', 'sub')), may hold values from -0.25 to 0.25
- current: float32 [65536], P(('leaf', 'sub')), may hold values from -6 to 6
- krylov_basis: float32 [8, 65536], P(None, ('leaf', 'sub')), may hold values from -0.0234375 to 0.0234375
- ritz_roots: float32 [2], replicated, may hold values from 40 to 400
- point_order: int32 [65536], P(('leaf', 'sub')), may hold values from 0 to 8191, as said below
- skeleton: int32 [128, 128], P(('leaf', 'sub')), may hold values from 0 to 511, as said below
- root_skeleton: int32 [8, 128], P('leaf'), may hold values from 0 to 8191, as said below
- near_list: int32 [128, 32], P(('leaf', 'sub')), may hold values from 0 to 47, as said below
- far_list: int32 [128, 4], P(('leaf', 'sub')), may hold values from 0 to 47, as said below
Outputs:
- orthogonal: float32 [65536], P(('leaf', 'sub'))
- hessenberg: float32 [9], replicated
The draws below stay inside these ranges and needn't reach their ends.
Inputs may be any that keep to these rules, and one draw needn't show every extreme that they name: Within each subtree (block of 8192 tree positions) point_order is a permutation of 0 to 8191. `skeleton`: each row holds 128 different point numbers of the leaf. `root_skeleton`: each row holds 128 different point numbers of the subtree. `near_list`: slots count 16 leaves of the previous subtree, then the own subtree, then the next one (circularly). The first slot of leaf a is its own, 16 + (a mod 16); the slots of a row are different, and no slot of a row is in the leaf's far_list. `far_list`: slots as in near_list; different within a row, never the leaf's own.
All inputs are finite; a program needn't handle non-finite values.
Results may differ from the reference program's by a relative error of at most 0.000096.
Values sent between devices are 32-bit elements; how exact they have to be, the bound alone decides.
A program may use at most 64 MiB of HBM per device.

```python
import math
import jax
import jax.numpy as jnp
from jax import lax

F = 64
LS = 512
SK = 128
NEAR = 32
FAR = 4
MB = 8
SUBLEAVES = 16
SUBTREES = 8
LEAVES = 128
NPTS = 65536


def slot_tables(key):
    base = jax.random.fold_in(key, 11)
    keys = jax.random.split(base, LEAVES)
    others = jax.vmap(lambda leafkey: jax.random.permutation(leafkey, 3 * SUBLEAVES - 1))(keys).astype(jnp.int32)
    own_slot = (SUBLEAVES + jnp.arange(LEAVES, dtype=jnp.int32) % SUBLEAVES)[:, None].astype(jnp.int32)
    shifted = jnp.where(others >= own_slot, others + 1, others).astype(jnp.int32)
    return (own_slot, shifted)


def draw_near_list(key, part):
    own_slot, shifted = slot_tables(key)
    return jnp.concatenate([own_slot, shifted[:, :NEAR - 1]], axis=1).astype(jnp.int32)


def draw_far_list(key, part):
    own_slot, shifted = slot_tables(key)
    return shifted[:, NEAR - 1:NEAR - 1 + FAR].astype(jnp.int32)


def draw_point_order(key, part):
    keys = jax.random.split(jax.random.fold_in(key, 23), SUBTREES)
    table = jax.vmap(lambda subkey: jax.random.permutation(subkey, SUBLEAVES * LS))(keys)
    return table.reshape(-1).astype(jnp.int32)


def draw_skeleton(key, part):
    keys = jax.random.split(jax.random.fold_in(key, 37), LEAVES)
    table = jax.vmap(lambda leafkey: jax.random.permutation(leafkey, LS)[:SK])(keys)
    return table.astype(jnp.int32)


def draw_root_skeleton(key, part):
    keys = jax.random.split(jax.random.fold_in(key, 41), SUBTREES)
    table = jax.vmap(lambda subkey: jax.random.permutation(subkey, SUBLEAVES * LS)[:SK])(keys)
    return table.astype(jnp.int32)


def levels(stream_key, dims, pieces, smallest, high):
    def one(axis_at, parts):
        heights = jax.random.uniform(jax.random.fold_in(jax.random.fold_in(stream_key, 6), axis_at), (parts,), jnp.float32, smallest / len(pieces), high / len(pieces))
        return jnp.repeat(jnp.exp(heights), dims[axis_at] // parts).reshape((-1,) + (1,) * (len(dims) - axis_at - 1))

    loudness = one(*pieces[0])
    for cut in pieces[1:]:
        loudness = loudness * one(*cut)
    return loudness


def scatter_about(own_key, extent, width, bound, shards=(), kind=jnp.bfloat16):
    values = width * jax.random.normal(own_key, extent, jnp.float32)
    if shards:
        values = values * levels(own_key, extent, shards, -0.22, 0.18)
    return jnp.clip(values, -bound, bound).astype(kind)


def setup_inputs(seed: int = 0) -> dict:
    streams_of = jax.random.split(jax.random.key(seed), 12)
    return {
        "points": scatter_about(streams_of[0], (NPTS, F), 1.0, 6.0, ((0, 32),), jnp.float32),
        "leaf_maps": scatter_about(streams_of[1], (LEAVES, SK, LS), LS ** -0.5, 0.25, ((0, 32),), jnp.float32),
        "root_maps": scatter_about(streams_of[2], (LEAVES, SK, LS), LS ** -0.5, 0.25, ((0, 32),), jnp.float32),
        "current": scatter_about(streams_of[3], (NPTS,), 1.0, 6.0, ((0, 32),), jnp.float32),
        "krylov_basis": scatter_about(streams_of[4], (MB, NPTS), NPTS ** -0.5, 0.0234375, ((1, 32),), jnp.float32),
        "ritz_roots": jnp.clip(jnp.exp(jax.random.uniform(streams_of[5], (2,), jnp.float32, math.log(40.0), math.log(400.0))), 40.0, 400.0),
        "point_order": draw_point_order(jax.random.fold_in(streams_of[11], 71), 0),
        "skeleton": draw_skeleton(jax.random.fold_in(streams_of[11], 71), 0),
        "root_skeleton": draw_root_skeleton(jax.random.fold_in(streams_of[11], 71), 0),
        "near_list": draw_near_list(jax.random.fold_in(streams_of[11], 71), 0),
        "far_list": draw_far_list(jax.random.fold_in(streams_of[11], 71), 0),
    }


HIGHEST_PREC = lax.Precision.HIGHEST
RIDGE_SHIFT = 1.0
EPSILON = 1e-06

def gaussian(inner_prod, target_sq, source_sq, feat_count):
    return jnp.exp(-(target_sq + source_sq - 2.0 * inner_prod) / feat_count)

def reference(points, leaf_maps, root_maps, current, krylov_basis, ritz_roots, point_order, skeleton, root_skeleton, near_list, far_list):
    feat_count = points.shape[1]
    leaf_points = points.reshape(LEAVES, LS, F)
    leaf_sq = lax.optimization_barrier(jnp.sum(leaf_points * leaf_points, axis=-1))
    skel_points = jnp.take_along_axis(leaf_points, skeleton[:, :, None], axis=1)
    skel_sq = lax.optimization_barrier(jnp.sum(skel_points * skel_points, axis=-1))
    subtree_of = (jnp.arange(LEAVES, dtype=jnp.int32) // SUBLEAVES).astype(jnp.int32)

    def to_global(window_slots):
        offset = window_slots // SUBLEAVES - 1
        return ((subtree_of[:, None] + offset) % SUBTREES * SUBLEAVES + window_slots % SUBLEAVES).astype(jnp.int32)
    near_global = to_global(near_list)
    far_global = to_global(far_list)
    far_points = skel_points[far_global]
    far_inner = jnp.einsum('bmf,bjnf->bjmn', skel_points, far_points, precision=HIGHEST_PREC)
    far_kernel = gaussian(far_inner, skel_sq[:, None, :, None], skel_sq[far_global][:, :, None, :], feat_count)
    subtree_points = points.reshape(SUBTREES, SUBLEAVES * LS, F)
    root_points = jnp.take_along_axis(subtree_points, root_skeleton[:, :, None], axis=1).reshape(SUBTREES * SK, F)
    root_sq = lax.optimization_barrier(jnp.sum(root_points * root_points, axis=-1))
    root_inner = jnp.dot(root_points, root_points.T, precision=HIGHEST_PREC)
    top_kernel = gaussian(root_inner, root_sq[:, None], root_sq[None, :], feat_count)
    distance = (jnp.arange(SUBTREES)[None, :] - jnp.arange(SUBTREES)[:, None]) % SUBTREES
    far_mask = (distance >= 1).astype(jnp.float32)
    top_kernel = top_kernel * jnp.repeat(jnp.repeat(far_mask, SK, axis=0), SK, axis=1)

    def operator(vector):
        values = vector.reshape(LEAVES, LS)
        skel_weights = jnp.einsum('bkn,bn->bk', leaf_maps, values, precision=HIGHEST_PREC)
        root_weights = jnp.einsum('bkn,bn->bk', root_maps, values, precision=HIGHEST_PREC).reshape(SUBTREES, SUBLEAVES, SK).sum(axis=1)

        def near_one(packed):
            targets, target_sq, neighbours = packed
            sources = leaf_points[neighbours]
            inner_prod = jnp.einsum('mf,jnf->jmn', targets, sources, precision=HIGHEST_PREC)
            kernel = gaussian(inner_prod, target_sq[None, :, None], leaf_sq[neighbours][:, None, :], feat_count)
            return jnp.einsum('jmn,jn->m', kernel, values[neighbours], precision=HIGHEST_PREC)
        result = lax.map(near_one, (leaf_points, leaf_sq, near_global))
        skel_out = jnp.einsum('bjmn,bjn->bm', far_kernel, skel_weights[far_global], precision=HIGHEST_PREC)
        result = result + jnp.einsum('bkn,bk->bn', leaf_maps, skel_out, precision=HIGHEST_PREC)
        root_out = jnp.dot(top_kernel, root_weights.reshape(-1), precision=HIGHEST_PREC).reshape(SUBTREES, SK)
        result = result + jnp.einsum('bkn,bk->bn', root_maps, root_out[subtree_of], precision=HIGHEST_PREC)
        return result.reshape(-1) + RIDGE_SHIFT * vector
    order_rows = point_order.reshape(SUBTREES, SUBLEAVES * LS)
    tree_vector = jnp.take_along_axis(current.reshape(SUBTREES, SUBLEAVES * LS), order_rows, axis=1).reshape(-1)
    first_section = tree_vector - operator(tree_vector) / ritz_roots[0]
    second = first_section - operator(first_section) / ritz_roots[1]
    preconditioned = (tree_vector - second).reshape(SUBTREES, SUBLEAVES * LS)
    user_grown = jax.vmap(lambda positions, entries: jnp.zeros_like(entries).at[positions].set(entries))(order_rows, preconditioned).reshape(-1)
    projections = jnp.dot(krylov_basis, user_grown, precision=HIGHEST_PREC)
    orthogonal = user_grown - jnp.dot(projections, krylov_basis, precision=HIGHEST_PREC)
    length_norm = jnp.sqrt(jnp.sum(orthogonal * orthogonal) + EPSILON)
    return (orthogonal, jnp.concatenate([projections, length_norm[None]]))
```

```python
import jax
import jax.numpy as jnp
from jax import lax
from jax.experimental import pallas as pl
from jax.experimental.pallas import tpu as pltpu
from jax.sharding import PartitionSpec as P

HIGHEST_PREC = lax.Precision.HIGHEST
RIDGE_SHIFT = 1.0
EPSILON = 1e-06


def with_halo(block, sides, width):
    for axis, dim in sides:
        count = lax.axis_size(axis)
        forward = [(i, i + 1) for i in range(count - 1)]
        forward.append((count - 1, 0))
        backward = [(target, source) for source, target in forward]
        low = lax.ppermute(
            lax.slice_in_dim(block, block.shape[dim] - width, None, axis=dim), axis, forward
        )
        high = lax.ppermute(lax.slice_in_dim(block, 0, width, axis=dim), axis, backward)
        block = jnp.concatenate([low, block, high], axis=dim)
    return block


def split3(x):
    a = x.astype(jnp.bfloat16)
    r = x - a.astype(jnp.float32)
    b = r.astype(jnp.bfloat16)
    c = (r - b.astype(jnp.float32)).astype(jnp.bfloat16)
    return a, b, c


def target_rows(own_points, scale):
    x = own_points * (2.0 * scale)
    hi = x.astype(jnp.bfloat16)
    lo = (x - hi.astype(jnp.float32)).astype(jnp.bfloat16)
    sq = -scale * jnp.sum(own_points * own_points, axis=-1, keepdims=True)
    a, b, c = split3(sq)
    one = jnp.ones_like(a)
    feat = own_points.shape[-1]
    pad = jnp.zeros(own_points.shape[:-1] + (feat - 6,), jnp.bfloat16)
    return jnp.concatenate([hi, lo, hi, one, one, one, a, b, c, pad], axis=-1)


def near_kernel(scale, near_ref, t_ref, w_ref, v_ref, out_ref, aug_ref, acc_ref):
    window, feat, size = w_ref.shape
    per_device = t_ref.shape[0]
    near_count = near_ref.shape[1]

    def build(i, carry):
        x = w_ref[i]
        hi = x.astype(jnp.bfloat16)
        lo = (x - hi.astype(jnp.float32)).astype(jnp.bfloat16)
        sq = -scale * jnp.sum(x * x, axis=0, keepdims=True)
        s1 = sq.astype(jnp.bfloat16).astype(jnp.float32)
        s2 = (sq - s1).astype(jnp.bfloat16).astype(jnp.float32)
        s3 = sq - s1 - s2
        row = lax.broadcasted_iota(jnp.int32, (feat, size), 0)
        extra = jnp.where(
            row == 0, s1, jnp.where(row == 1, s2, jnp.where(row == 2, s3, jnp.where(row < 6, 1.0, 0.0)))
        )
        aug_ref[i, pl.ds(0, feat)] = hi
        aug_ref[i, pl.ds(feat, feat)] = hi
        aug_ref[i, pl.ds(2 * feat, feat)] = lo
        aug_ref[i, pl.ds(3 * feat, feat)] = extra.astype(jnp.bfloat16)
        return carry

    lax.fori_loop(0, window, build, 0)
    for b in range(per_device):
        acc_ref[...] = jnp.zeros_like(acc_ref)

        def step(s, carry):
            slot = near_ref[b, s]
            inner = jnp.dot(t_ref[b], aug_ref[slot], preferred_element_type=jnp.float32)
            prod = jnp.exp2(inner) * v_ref[slot]
            total = prod[:, 0:128]
            for g in range(1, size // 128):
                total = total + prod[:, g * 128 : (g + 1) * 128]
            acc_ref[...] += total
            return carry

        lax.fori_loop(0, near_count, step, 0)
        out_ref[b] = acc_ref[...]


def near_apply(near_list, targets, window_t, values, scale):
    per_device, size, width = targets.shape
    window, feat, _ = window_t.shape
    vmem = pl.BlockSpec(memory_space=pltpu.VMEM)
    part = pl.pallas_call(
        lambda *refs: near_kernel(scale, *refs),
        out_shape=jax.ShapeDtypeStruct((per_device, size, 128), jnp.float32),
        in_specs=[pl.BlockSpec(memory_space=pltpu.SMEM), vmem, vmem, vmem],
        out_specs=vmem,
        scratch_shapes=[
            pltpu.VMEM((window, width, size), jnp.bfloat16),
            pltpu.VMEM((size, 128), jnp.float32),
        ],
        compiler_params=pltpu.CompilerParams(vmem_limit_bytes=48 * 1024 * 1024),
        name="near",
    )(near_list, targets, window_t, values)
    return jnp.sum(part, axis=-1)


def gaussian(inner_prod, target_sq, source_sq, feat_count):
    return jnp.exp(-(target_sq + source_sq - 2.0 * inner_prod) / feat_count)


def shards(
    points,
    leaf_maps,
    root_maps,
    current,
    krylov_basis,
    ritz_roots,
    point_order,
    skeleton,
    root_skeleton,
    near_list,
    far_list,
):
    per_device, skel_count, leaf_size = leaf_maps.shape
    feat_count = points.shape[1]
    sub_count = lax.axis_size("sub")
    sub_leaves = per_device * sub_count
    leaf_count = lax.axis_size("leaf")
    leaf_index = lax.axis_index("leaf")
    own_points = points.reshape(per_device, leaf_size, feat_count)
    skel_points = jnp.take_along_axis(own_points, skeleton[:, :, None], axis=1)
    skel_sq = jnp.sum(skel_points * skel_points, axis=-1)
    leaf_data = jnp.concatenate([own_points, skel_points], axis=1).transpose(0, 2, 1)
    subtree_data = lax.all_gather(leaf_data, "sub", axis=0, tiled=True)
    window_data = with_halo(subtree_data, (("leaf", 0),), sub_leaves)
    window_t = window_data[:, :, :leaf_size]
    scale = 1.4426950408889634 / feat_count
    targets = target_rows(own_points, scale)
    far_points = window_data[:, :, leaf_size:][far_list].transpose(0, 1, 3, 2)
    far_inner = jnp.einsum("bmf,bjnf->bjmn", skel_points, far_points, precision=HIGHEST_PREC)
    far_kernel = gaussian(
        far_inner,
        skel_sq[:, None, :, None],
        jnp.sum(far_points * far_points, axis=-1)[:, :, None, :],
        feat_count,
    )
    subtree_points = subtree_data[:, :, :leaf_size]
    root_index = root_skeleton[0]
    own_root = subtree_points[root_index // leaf_size, :, root_index % leaf_size]
    all_roots = lax.all_gather(own_root[None], "leaf", axis=0, tiled=True).reshape(
        leaf_count * skel_count, feat_count
    )
    own_root_sq = jnp.sum(own_root * own_root, axis=-1)
    all_root_sq = jnp.sum(all_roots * all_roots, axis=-1)
    top_inner = jnp.dot(own_root, all_roots.T, precision=HIGHEST_PREC)
    top_kernel = gaussian(top_inner, own_root_sq[:, None], all_root_sq[None, :], feat_count)
    distance = (jnp.arange(leaf_count, dtype=jnp.int32) - leaf_index) % leaf_count
    far_mask = (distance >= 1).astype(jnp.float32)
    top_kernel = top_kernel * jnp.repeat(far_mask, skel_count)[None, :]
    def operator(vector):
        values = vector.reshape(per_device, leaf_size)
        skel_weights = jnp.einsum("bkn,bn->bk", leaf_maps, values, precision=HIGHEST_PREC)
        root_part = jnp.einsum("bkn,bn->k", root_maps, values, precision=HIGHEST_PREC)
        packed = jnp.concatenate([values, skel_weights], axis=1)
        subtree_values = lax.all_gather(packed, "sub", axis=0, tiled=True)
        window_values = with_halo(subtree_values, (("leaf", 0),), sub_leaves)
        root_total = lax.psum(root_part, "sub")
        root_weights = lax.all_gather(root_total[None], "leaf", axis=0, tiled=True)
        window_entries = window_values[:, :leaf_size]

        result = near_apply(near_list, targets, window_t, window_entries[:, None, :], scale)
        skel_out = jnp.einsum(
            "bjmn,bjn->bm",
            far_kernel,
            window_values[far_list][:, :, leaf_size:],
            precision=HIGHEST_PREC,
        )
        result = result + jnp.einsum("bkn,bk->bn", leaf_maps, skel_out, precision=HIGHEST_PREC)
        root_out = jnp.dot(top_kernel, root_weights.reshape(-1), precision=HIGHEST_PREC)
        result = result + jnp.einsum("bkn,k->bn", root_maps, root_out, precision=HIGHEST_PREC)
        return result.reshape(-1) + RIDGE_SHIFT * vector

    user_subtree = lax.all_gather(current, "sub", axis=0, tiled=True)
    tree_vector = jnp.take(user_subtree, point_order, axis=0)
    first_section = tree_vector - operator(tree_vector) / ritz_roots[0]
    second = first_section - operator(first_section) / ritz_roots[1]
    preconditioned = tree_vector - second
    placed = jnp.zeros((sub_leaves * leaf_size,), jnp.float32).at[point_order].set(preconditioned)
    user_grown = lax.psum_scatter(placed, "sub", scatter_dimension=0, tiled=True)
    local_proj = jnp.dot(krylov_basis, user_grown, precision=HIGHEST_PREC)
    local_gram = jnp.dot(krylov_basis, krylov_basis.T, precision=HIGHEST_PREC)
    projections, squares, gram_matrix = lax.psum(
        (local_proj, jnp.sum(user_grown * user_grown), local_gram), ("leaf", "sub")
    )
    orthogonal = user_grown - jnp.dot(projections, krylov_basis, precision=HIGHEST_PREC)
    length_sq = (
        squares
        - 2.0 * jnp.dot(projections, projections, precision=HIGHEST_PREC)
        + jnp.dot(
            projections,
            jnp.dot(gram_matrix, projections, precision=HIGHEST_PREC),
            precision=HIGHEST_PREC,
        )
    )
    length_norm = jnp.sqrt(length_sq + EPSILON)
    return (orthogonal, jnp.concatenate([projections, length_norm[None]]))


def solution(mesh):
    return jax.shard_map(
        shards,
        mesh=mesh,
        in_specs=(
            P(("leaf", "sub"), None),
            P(("leaf", "sub"), None, None),
            P(("leaf", "sub"), None, None),
            P(("leaf", "sub")),
            P(None, ("leaf", "sub")),
            P(),
            P(("leaf", "sub")),
            P(("leaf", "sub"), None),
            P("leaf", None),
            P(("leaf", "sub"), None),
            P(("leaf", "sub"), None),
        ),
        out_specs=(P(("leaf", "sub")), P()),
        check_vma=False,
    )
```

```python
import jax
import jax.numpy as jnp
from jax import lax
from jax.experimental import pallas as pl
from jax.experimental.pallas import tpu as pltpu
from jax.sharding import PartitionSpec as P

HIGHEST_PREC = lax.Precision.HIGHEST
RIDGE_SHIFT = 1.0
EPSILON = 1e-06


MESH = pl.DeviceIdType.MESH
VMEM = pl.BlockSpec(memory_space=pltpu.VMEM)


def position():
    return (
        lax.axis_index("leaf"),
        lax.axis_index("sub"),
        lax.axis_size("leaf"),
        lax.axis_size("sub"),
    )


def greet(peers):
    leaf, sub, leaf_count, sub_count = position()
    barrier = pltpu.get_barrier_semaphore()
    for dl, ds in peers:
        there = (lax.rem(leaf + dl, leaf_count), lax.rem(sub + ds, sub_count))
        pl.semaphore_signal(barrier, inc=1, device_id=there, device_id_type=MESH)
    pl.semaphore_wait(barrier, len(peers))


class Channel:
    def __init__(self, block, lead, peers, slot, per_target=False):
        self.block, self.peers, self.slot, self.per_target = block, peers, slot, per_target
        shape = block.shape[1:] if per_target else block.shape
        self.out = jax.ShapeDtypeStruct(tuple(lead) + shape, block.dtype)


def exchange(channels, collective_id):
    count = len(channels)
    greeted = sorted({peer for channel in channels for peer in channel.peers})

    def kernel(*refs):
        leaf, sub, leaf_count, sub_count = position()
        ins, outs = refs[:count], refs[count : 2 * count]
        sems = refs[2 * count :]
        greet(greeted)
        started = []
        for c, channel in enumerate(channels):
            send, recv = sems[2 * c], sems[2 * c + 1]
            for k, (dl, ds) in enumerate(channel.peers):
                there = (lax.rem(leaf + dl, leaf_count), lax.rem(sub + ds, sub_count))
                source = ins[c].at[there[1]] if channel.per_target else ins[c]
                copy = pltpu.make_async_remote_copy(
                    src_ref=source,
                    dst_ref=outs[c].at[channel.slot(leaf, sub, dl, sub_count)],
                    send_sem=send.at[k],
                    recv_sem=recv.at[k],
                    device_id=there,
                    device_id_type=MESH,
                )
                copy.start()
                started.append(copy)
        for c, channel in enumerate(channels):
            own = ins[c][sub] if channel.per_target else ins[c][...]
            outs[c][channel.slot(leaf, sub, 0, sub_count)] = own
        for copy in started:
            copy.wait_send()
        for c, channel in enumerate(channels):
            send, recv = sems[2 * c], sems[2 * c + 1]
            for k, (dl, ds) in enumerate(channel.peers):
                here = (
                    lax.rem(leaf + leaf_count - dl, leaf_count),
                    lax.rem(sub + sub_count - ds, sub_count),
                )
                slot = channel.slot(here[0], here[1], dl, sub_count)
                pltpu.make_async_remote_copy(
                    src_ref=outs[c].at[slot],
                    dst_ref=outs[c].at[slot],
                    send_sem=send.at[k],
                    recv_sem=recv.at[k],
                    device_id=here,
                    device_id_type=MESH,
                ).wait_recv()

    scratch = []
    for channel in channels:
        scratch += [pltpu.SemaphoreType.DMA((len(channel.peers),))] * 2
    return pl.pallas_call(
        kernel,
        out_shape=[channel.out for channel in channels],
        in_specs=[VMEM] * count,
        out_specs=[VMEM] * count,
        scratch_shapes=scratch,
        compiler_params=pltpu.CompilerParams(collective_id=collective_id, has_side_effects=True),
        name="exchange",
    )(*[channel.block for channel in channels])


def sub_peers():
    return [(0, ds) for ds in range(1, lax.axis_size("sub"))]


def leaf_peers():
    return [(dl, 0) for dl in range(1, lax.axis_size("leaf"))]


def all_peers():
    subs = lax.axis_size("sub")
    return [(dl, ds) for dl in range(lax.axis_size("leaf")) for ds in range(subs) if dl or ds]


def window_peers():
    subs, leaves = lax.axis_size("sub"), lax.axis_size("leaf")
    return [(dl, ds) for dl in (0, 1, leaves - 1) for ds in range(subs) if dl or ds]


def sub_slot(leaf, sub, dl, sub_count):
    return sub


def leaf_slot(leaf, sub, dl, sub_count):
    return leaf


def all_slot(leaf, sub, dl, sub_count):
    return leaf * sub_count + sub


def window_slot(leaf, sub, dl, sub_count):
    part = 1 if dl == 0 else (0 if dl == 1 else 2)
    return part * sub_count + sub


def gather_window(block, collective_id):
    subs, leaves = lax.axis_size("sub"), lax.axis_size("leaf")
    chips = subs // 2
    hops = [(1, 0), (leaves - 1, 0)]

    def kernel(x_ref, out_ref, halo_send, recv, chip_send, core_send):
        leaf, sub, leaf_count, sub_count = position()
        chip, core = sub // 2, lax.rem(sub, 2)
        other = chip * 2 + 1 - core
        greet([(0, ds) for ds in range(1, subs)] + hops)

        def remote(source, part, owner, send, there):
            return pltpu.make_async_remote_copy(
                src_ref=source,
                dst_ref=out_ref.at[part * sub_count + owner],
                send_sem=send,
                recv_sem=recv.at[part * sub_count + owner],
                device_id=there,
                device_id_type=MESH,
            )

        def arrived(part, owner):
            block_ref = out_ref.at[part * sub_count + owner]
            remote(block_ref, part, owner, core_send.at[0], (leaf, other)).wait_recv()

        started = []

        def start(copy):
            copy.start()
            started.append(copy)

        def spread(part, source):
            for k in range(1, chips):
                there = lax.rem(chip + k, chips) * 2 + core
                start(remote(source, part, sub, chip_send.at[part * chips + k], (leaf, there)))
            start(remote(source, part, sub, core_send.at[part * chips], (leaf, other)))

        for j, (dl, part) in enumerate(((1, 0), (leaves - 1, 2))):
            there = lax.rem(leaf + dl, leaf_count)
            start(remote(x_ref, part, sub, halo_send.at[j], (there, sub)))
        spread(1, x_ref)
        out_ref[sub_count + sub] = x_ref[...]

        def forward(part):
            for k in range(1, chips):
                owner = lax.rem(chip + chips - k, chips) * 2 + core
                arrived(part, owner)
                start(
                    remote(
                        out_ref.at[part * sub_count + owner],
                        part,
                        owner,
                        core_send.at[part * chips + k],
                        (leaf, other),
                    )
                )

        for part in (0, 2):
            arrived(part, sub)
            spread(part, out_ref.at[part * sub_count + sub])
        for part in (1, 0, 2):
            forward(part)
        for part in range(3):
            for k in range(chips):
                arrived(part, lax.rem(chip + k, chips) * 2 + 1 - core)
        for copy in started:
            copy.wait_send()

    return pl.pallas_call(
        kernel,
        out_shape=jax.ShapeDtypeStruct((3 * subs,) + block.shape, block.dtype),
        in_specs=[VMEM],
        out_specs=VMEM,
        scratch_shapes=[
            pltpu.SemaphoreType.DMA((2,)),
            pltpu.SemaphoreType.DMA((3 * subs,)),
            pltpu.SemaphoreType.DMA((3 * chips,)),
            pltpu.SemaphoreType.DMA((3 * chips,)),
        ],
        compiler_params=pltpu.CompilerParams(
            collective_id=collective_id, has_side_effects=True, vmem_limit_bytes=24 * 1024 * 1024
        ),
        name="gather_window",
    )(block)


def split3(x):
    a = x.astype(jnp.bfloat16)
    r = x - a.astype(jnp.float32)
    b = r.astype(jnp.bfloat16)
    c = (r - b.astype(jnp.float32)).astype(jnp.bfloat16)
    return a, b, c


def target_rows(own_points, scale):
    x = own_points * (2.0 * scale)
    hi = x.astype(jnp.bfloat16)
    lo = (x - hi.astype(jnp.float32)).astype(jnp.bfloat16)
    sq = -scale * jnp.sum(own_points * own_points, axis=-1, keepdims=True)
    a, b, c = split3(sq)
    one = jnp.ones_like(a)
    feat = own_points.shape[-1]
    pad = jnp.zeros(own_points.shape[:-1] + (feat - 6,), jnp.bfloat16)
    return jnp.concatenate([hi, lo, hi, one, one, one, a, b, c, pad], axis=-1)


def near_kernel(scale, near_ref, t_ref, w_ref, v_ref, out_ref, aug_ref, acc_ref):
    window, feat, size = w_ref.shape
    per_device = t_ref.shape[0]
    near_count = near_ref.shape[1]

    def build(i, carry):
        x = w_ref[i]
        hi = x.astype(jnp.bfloat16)
        lo = (x - hi.astype(jnp.float32)).astype(jnp.bfloat16)
        sq = -scale * jnp.sum(x * x, axis=0, keepdims=True)
        s1 = sq.astype(jnp.bfloat16).astype(jnp.float32)
        s2 = (sq - s1).astype(jnp.bfloat16).astype(jnp.float32)
        s3 = sq - s1 - s2
        row = lax.broadcasted_iota(jnp.int32, (feat, size), 0)
        extra = jnp.where(
            row == 0, s1, jnp.where(row == 1, s2, jnp.where(row == 2, s3, jnp.where(row < 6, 1.0, 0.0)))
        )
        aug_ref[i, pl.ds(0, feat)] = hi
        aug_ref[i, pl.ds(feat, feat)] = hi
        aug_ref[i, pl.ds(2 * feat, feat)] = lo
        aug_ref[i, pl.ds(3 * feat, feat)] = extra.astype(jnp.bfloat16)
        return carry

    lax.fori_loop(0, window, build, 0)
    for b in range(per_device):
        acc_ref[...] = jnp.zeros_like(acc_ref)

        def step(s, carry):
            slot = near_ref[b, s]
            inner = jnp.dot(t_ref[b], aug_ref[slot], preferred_element_type=jnp.float32)
            prod = jnp.exp2(inner) * v_ref[slot]
            total = prod[:, 0:128]
            for g in range(1, size // 128):
                total = total + prod[:, g * 128 : (g + 1) * 128]
            acc_ref[...] += total
            return carry

        lax.fori_loop(0, near_count, step, 0)
        out_ref[b] = acc_ref[...]


def near_apply(near_list, targets, window_t, values, scale):
    per_device, size, width = targets.shape
    window, feat, _ = window_t.shape
    vmem = pl.BlockSpec(memory_space=pltpu.VMEM)
    part = pl.pallas_call(
        lambda *refs: near_kernel(scale, *refs),
        out_shape=jax.ShapeDtypeStruct((per_device, size, 128), jnp.float32),
        in_specs=[pl.BlockSpec(memory_space=pltpu.SMEM), vmem, vmem, vmem],
        out_specs=vmem,
        scratch_shapes=[
            pltpu.VMEM((window, width, size), jnp.bfloat16),
            pltpu.VMEM((size, 128), jnp.float32),
        ],
        compiler_params=pltpu.CompilerParams(vmem_limit_bytes=48 * 1024 * 1024),
        name="near",
    )(near_list, targets, window_t, values)
    return jnp.sum(part, axis=-1)


def gaussian(inner_prod, target_sq, source_sq, feat_count):
    return jnp.exp(-(target_sq + source_sq - 2.0 * inner_prod) / feat_count)


def shards(
    points,
    leaf_maps,
    root_maps,
    current,
    krylov_basis,
    ritz_roots,
    point_order,
    skeleton,
    root_skeleton,
    near_list,
    far_list,
):
    per_device, skel_count, leaf_size = leaf_maps.shape
    feat_count = points.shape[1]
    sub_count = lax.axis_size("sub")
    sub_leaves = per_device * sub_count
    leaf_count = lax.axis_size("leaf")
    leaf_index = lax.axis_index("leaf")
    own_points = points.reshape(per_device, leaf_size, feat_count)
    own_t = own_points.transpose(0, 2, 1)
    window_t = gather_window(own_t, 1).reshape(3 * sub_leaves, feat_count, leaf_size)
    scale = 1.4426950408889634 / feat_count
    targets = target_rows(own_points, scale)

    def pick(points_t, index):
        chosen = index[..., None, :] == jnp.arange(leaf_size, dtype=jnp.int32)[:, None]
        return jnp.einsum(
            "...fn,...nk->...kf", points_t, chosen.astype(jnp.float32), precision=HIGHEST_PREC
        )

    lanes = 128
    rows = sub_leaves * leaf_size // lanes
    in_row = point_order[:, None] // lanes == jnp.arange(rows, dtype=jnp.int32)[None, :]
    in_lane = point_order[:, None] % lanes == jnp.arange(lanes, dtype=jnp.int32)[None, :]
    in_row, in_lane = in_row.astype(jnp.float32), in_lane.astype(jnp.float32)
    own_rows = per_device * leaf_size // lanes
    user_subtree, slot_index = exchange(
        [
            Channel(current.reshape(own_rows, lanes), (sub_count,), sub_peers(), sub_slot),
            Channel(
                skeleton.astype(jnp.float32), (3 * sub_count,), window_peers(), window_slot
            ),
        ],
        2,
    )
    window_skel = slot_index.reshape(3 * sub_leaves, skel_count).astype(jnp.int32)
    picked = jnp.dot(in_row, user_subtree.reshape(rows, lanes), precision=HIGHEST_PREC)
    tree_vector = jnp.sum(picked * in_lane, axis=1)

    skel_points = pick(own_t, skeleton)
    skel_sq = jnp.sum(skel_points * skel_points, axis=-1)
    far_points = pick(window_t[far_list], window_skel[far_list])
    far_inner = jnp.einsum("bmf,bjnf->bjmn", skel_points, far_points, precision=HIGHEST_PREC)
    far_kernel = gaussian(
        far_inner,
        skel_sq[:, None, :, None],
        jnp.sum(far_points * far_points, axis=-1)[:, :, None, :],
        feat_count,
    )
    subtree_points = window_t[sub_leaves : 2 * sub_leaves]
    root_index = root_skeleton[0]
    own_root = subtree_points[root_index // leaf_size, :, root_index % leaf_size]
    (all_roots_t,) = exchange([Channel(own_root.T, (leaf_count,), leaf_peers(), leaf_slot)], 3)
    all_roots = all_roots_t.transpose(0, 2, 1).reshape(leaf_count * skel_count, feat_count)
    own_root_sq = jnp.sum(own_root * own_root, axis=-1)
    all_root_sq = jnp.sum(all_roots * all_roots, axis=-1)
    top_inner = jnp.dot(own_root, all_roots.T, precision=HIGHEST_PREC)
    top_kernel = gaussian(top_inner, own_root_sq[:, None], all_root_sq[None, :], feat_count)
    distance = (jnp.arange(leaf_count, dtype=jnp.int32) - leaf_index) % leaf_count
    far_mask = (distance >= 1).astype(jnp.float32)
    top_kernel = top_kernel * jnp.repeat(far_mask, skel_count)[None, :]
    def operator(vector):
        values = vector.reshape(per_device, leaf_size)
        skel_weights = jnp.einsum("bkn,bn->bk", leaf_maps, values, precision=HIGHEST_PREC)
        root_part = jnp.einsum("bkn,bn->k", root_maps, values, precision=HIGHEST_PREC)
        packed = jnp.concatenate([values, skel_weights], axis=1)
        window_values, root_parts = exchange(
            [
                Channel(packed, (3 * sub_count,), window_peers(), window_slot),
                Channel(root_part[None], (leaf_count * sub_count,), all_peers(), all_slot),
            ],
            4,
        )
        window_values = window_values.reshape(3 * sub_leaves, leaf_size + skel_count)
        root_weights = jnp.sum(root_parts.reshape(leaf_count, sub_count, skel_count), axis=1)
        window_entries = window_values[:, :leaf_size]

        result = near_apply(near_list, targets, window_t, window_entries[:, None, :], scale)
        skel_out = jnp.einsum(
            "bjmn,bjn->bm",
            far_kernel,
            window_values[far_list][:, :, leaf_size:],
            precision=HIGHEST_PREC,
        )
        result = result + jnp.einsum("bkn,bk->bn", leaf_maps, skel_out, precision=HIGHEST_PREC)
        root_out = jnp.dot(top_kernel, root_weights.reshape(-1), precision=HIGHEST_PREC)
        result = result + jnp.einsum("bkn,k->bn", root_maps, root_out, precision=HIGHEST_PREC)
        return result.reshape(-1) + RIDGE_SHIFT * vector

    first_section = tree_vector - operator(tree_vector) / ritz_roots[0]
    second = first_section - operator(first_section) / ritz_roots[1]
    preconditioned = tree_vector - second
    placed = jnp.einsum(
        "ir,il->rl", in_row, preconditioned[:, None] * in_lane, precision=HIGHEST_PREC
    ).reshape(sub_count, own_rows, lanes)
    (pieces,) = exchange([Channel(placed, (sub_count,), sub_peers(), sub_slot, True)], 5)
    user_grown = jnp.sum(pieces, axis=0).reshape(-1)
    local_proj = jnp.dot(krylov_basis, user_grown, precision=HIGHEST_PREC)
    local_gram = jnp.dot(krylov_basis, krylov_basis.T, precision=HIGHEST_PREC)
    basis_count = local_proj.shape[0]
    square = jnp.sum(user_grown * user_grown)
    totals = jnp.concatenate([local_proj, square[None], local_gram.reshape(-1)])
    width = -(-totals.shape[0] // lanes) * lanes
    totals = jnp.pad(totals, (0, width - totals.shape[0]))
    (every,) = exchange(
        [Channel(totals[None], (leaf_count * sub_count,), all_peers(), all_slot)], 6
    )
    totals = jnp.sum(every, axis=(0, 1))
    projections, squares = totals[:basis_count], totals[basis_count]
    gram_matrix = totals[basis_count + 1 : basis_count + 1 + basis_count * basis_count]
    gram_matrix = gram_matrix.reshape(basis_count, basis_count)
    orthogonal = user_grown - jnp.dot(projections, krylov_basis, precision=HIGHEST_PREC)
    length_sq = (
        squares
        - 2.0 * jnp.dot(projections, projections, precision=HIGHEST_PREC)
        + jnp.dot(
            projections,
            jnp.dot(gram_matrix, projections, precision=HIGHEST_PREC),
            precision=HIGHEST_PREC,
        )
    )
    length_norm = jnp.sqrt(length_sq + EPSILON)
    return (orthogonal, jnp.concatenate([projections, length_norm[None]]))


def solution(mesh):
    return jax.shard_map(
        shards,
        mesh=mesh,
        in_specs=(
            P(("leaf", "sub"), None),
            P(("leaf", "sub"), None, None),
            P(("leaf", "sub"), None, None),
            P(("leaf", "sub")),
            P(None, ("leaf", "sub")),
            P(),
            P(("leaf", "sub")),
            P(("leaf", "sub"), None),
            P("leaf", None),
            P(("leaf", "sub"), None),
            P(("leaf", "sub"), None),
        ),
        out_specs=(P(("leaf", "sub")), P()),
        check_vma=False,
    )
```

```python
import jax
import jax.numpy as jnp
from jax import lax
from jax.experimental import pallas as pl
from jax.experimental.pallas import tpu as pltpu
from jax.sharding import PartitionSpec as P

HIGHEST_PREC = lax.Precision.HIGHEST
RIDGE_SHIFT = 1.0
EPSILON = 1e-06


CHUNK = 512
UNROLL = 16
MESH = pl.DeviceIdType.MESH
VMEM = pl.BlockSpec(memory_space=pltpu.VMEM)


def position():
    return (
        lax.axis_index("leaf"),
        lax.axis_index("sub"),
        lax.axis_size("leaf"),
        lax.axis_size("sub"),
    )


def greet(peers):
    leaf, sub, leaf_count, sub_count = position()
    barrier = pltpu.get_barrier_semaphore()
    for dl, ds in peers:
        there = (lax.rem(leaf + dl, leaf_count), lax.rem(sub + ds, sub_count))
        pl.semaphore_signal(barrier, inc=1, device_id=there, device_id_type=MESH)
    pl.semaphore_wait(barrier, len(peers))


class Channel:
    def __init__(self, block, lead, peers, slot, per_target=False):
        self.block, self.peers, self.slot, self.per_target = block, peers, slot, per_target
        shape = block.shape[1:] if per_target else block.shape
        self.out = jax.ShapeDtypeStruct(tuple(lead) + shape, block.dtype)


def exchange(channels, collective_id):
    count = len(channels)
    greeted = sorted({peer for channel in channels for peer in channel.peers})

    def kernel(*refs):
        leaf, sub, leaf_count, sub_count = position()
        ins, outs = refs[:count], refs[count : 2 * count]
        sems = refs[2 * count :]
        greet(greeted)
        started = []
        for c, channel in enumerate(channels):
            send, recv = sems[2 * c], sems[2 * c + 1]
            for k, (dl, ds) in enumerate(channel.peers):
                there = (lax.rem(leaf + dl, leaf_count), lax.rem(sub + ds, sub_count))
                source = ins[c].at[there[1]] if channel.per_target else ins[c]
                copy = pltpu.make_async_remote_copy(
                    src_ref=source,
                    dst_ref=outs[c].at[channel.slot(leaf, sub, dl, sub_count)],
                    send_sem=send.at[k],
                    recv_sem=recv.at[k],
                    device_id=there,
                    device_id_type=MESH,
                )
                copy.start()
                started.append(copy)
        for c, channel in enumerate(channels):
            own = ins[c][sub] if channel.per_target else ins[c][...]
            outs[c][channel.slot(leaf, sub, 0, sub_count)] = own
        for copy in started:
            copy.wait_send()
        for c, channel in enumerate(channels):
            send, recv = sems[2 * c], sems[2 * c + 1]
            for k, (dl, ds) in enumerate(channel.peers):
                here = (
                    lax.rem(leaf + leaf_count - dl, leaf_count),
                    lax.rem(sub + sub_count - ds, sub_count),
                )
                slot = channel.slot(here[0], here[1], dl, sub_count)
                pltpu.make_async_remote_copy(
                    src_ref=outs[c].at[slot],
                    dst_ref=outs[c].at[slot],
                    send_sem=send.at[k],
                    recv_sem=recv.at[k],
                    device_id=here,
                    device_id_type=MESH,
                ).wait_recv()

    scratch = []
    for channel in channels:
        scratch += [pltpu.SemaphoreType.DMA((len(channel.peers),))] * 2
    return pl.pallas_call(
        kernel,
        out_shape=[channel.out for channel in channels],
        in_specs=[VMEM] * count,
        out_specs=[VMEM] * count,
        scratch_shapes=scratch,
        compiler_params=pltpu.CompilerParams(collective_id=collective_id, has_side_effects=True),
        name="exchange",
    )(*[channel.block for channel in channels])


def sub_peers():
    return [(0, ds) for ds in range(1, lax.axis_size("sub"))]


def leaf_peers():
    return [(dl, 0) for dl in range(1, lax.axis_size("leaf"))]


def all_peers():
    subs = lax.axis_size("sub")
    return [(dl, ds) for dl in range(lax.axis_size("leaf")) for ds in range(subs) if dl or ds]


def window_peers():
    subs, leaves = lax.axis_size("sub"), lax.axis_size("leaf")
    return [(dl, ds) for dl in (0, 1, leaves - 1) for ds in range(subs) if dl or ds]


def sub_slot(leaf, sub, dl, sub_count):
    return sub


def leaf_slot(leaf, sub, dl, sub_count):
    return leaf


def all_slot(leaf, sub, dl, sub_count):
    return leaf * sub_count + sub


def window_slot(leaf, sub, dl, sub_count):
    part = 1 if dl == 0 else (0 if dl == 1 else 2)
    return part * sub_count + sub


def gather_window(block, collective_id):
    subs, leaves = lax.axis_size("sub"), lax.axis_size("leaf")
    chips = subs // 2
    hops = [(1, 0), (leaves - 1, 0)]

    def kernel(x_ref, out_ref, halo_send, recv, chip_send, core_send):
        leaf, sub, leaf_count, sub_count = position()
        chip, core = sub // 2, lax.rem(sub, 2)
        other = chip * 2 + 1 - core
        greet([(0, ds) for ds in range(1, subs)] + hops)

        def remote(source, part, owner, send, there):
            return pltpu.make_async_remote_copy(
                src_ref=source,
                dst_ref=out_ref.at[part * sub_count + owner],
                send_sem=send,
                recv_sem=recv.at[part * sub_count + owner],
                device_id=there,
                device_id_type=MESH,
            )

        def arrived(part, owner):
            block_ref = out_ref.at[part * sub_count + owner]
            remote(block_ref, part, owner, core_send.at[0], (leaf, other)).wait_recv()

        started = []

        def start(copy):
            copy.start()
            started.append(copy)

        def spread(part, source):
            for k in range(1, chips):
                there = lax.rem(chip + k, chips) * 2 + core
                start(remote(source, part, sub, chip_send.at[part * chips + k], (leaf, there)))
            start(remote(source, part, sub, core_send.at[part * chips], (leaf, other)))

        for j, (dl, part) in enumerate(((1, 0), (leaves - 1, 2))):
            there = lax.rem(leaf + dl, leaf_count)
            start(remote(x_ref, part, sub, halo_send.at[j], (there, sub)))
        spread(1, x_ref)
        out_ref[sub_count + sub] = x_ref[...]

        def forward(part):
            for k in range(1, chips):
                owner = lax.rem(chip + chips - k, chips) * 2 + core
                arrived(part, owner)
                start(
                    remote(
                        out_ref.at[part * sub_count + owner],
                        part,
                        owner,
                        core_send.at[part * chips + k],
                        (leaf, other),
                    )
                )

        for part in (0, 2):
            arrived(part, sub)
            spread(part, out_ref.at[part * sub_count + sub])
        for part in (1, 0, 2):
            forward(part)
        for part in range(3):
            for k in range(chips):
                arrived(part, lax.rem(chip + k, chips) * 2 + 1 - core)
        for copy in started:
            copy.wait_send()

    return pl.pallas_call(
        kernel,
        out_shape=jax.ShapeDtypeStruct((3 * subs,) + block.shape, block.dtype),
        in_specs=[VMEM],
        out_specs=VMEM,
        scratch_shapes=[
            pltpu.SemaphoreType.DMA((2,)),
            pltpu.SemaphoreType.DMA((3 * subs,)),
            pltpu.SemaphoreType.DMA((3 * chips,)),
            pltpu.SemaphoreType.DMA((3 * chips,)),
        ],
        compiler_params=pltpu.CompilerParams(
            collective_id=collective_id, has_side_effects=True, vmem_limit_bytes=24 * 1024 * 1024
        ),
        name="gather_window",
    )(block)


def augmented(x, scale, target):
    feat, size = x.shape
    sq = -scale * jnp.sum(x * x, axis=0, keepdims=True)
    s1 = sq.astype(jnp.bfloat16).astype(jnp.float32)
    s2 = (sq - s1).astype(jnp.bfloat16).astype(jnp.float32)
    s3 = sq - s1 - s2
    row = lax.broadcasted_iota(jnp.int32, (feat, size), 0)
    first = 3 if target else 0
    ones = jnp.where(row < 6, 1.0, 0.0)
    extra = jnp.where(
        row == first,
        s1,
        jnp.where(row == first + 1, s2, jnp.where(row == first + 2, s3, ones)),
    )
    if target:
        x = x * (2.0 * scale)
    hi = x.astype(jnp.bfloat16).astype(jnp.float32)
    lo = x - hi
    return (hi, lo, hi, extra) if target else (hi, hi, lo, extra)


def near_kernel(scale, near_ref, own_ref, w_ref, v_ref, out_ref, aug_ref, t_ref, acc_ref):
    window, feat, size = w_ref.shape
    per_device = own_ref.shape[0]
    near_count = near_ref.shape[1]

    def build(i, carry):
        for k, piece in enumerate(augmented(w_ref[i], scale, False)):
            aug_ref[i, pl.ds(k * feat, feat)] = piece.astype(jnp.bfloat16)
        return carry

    lax.fori_loop(0, window, build, 0)
    for b in range(per_device):
        acc_ref[...] = jnp.zeros_like(acc_ref)
        pieces = augmented(own_ref[b], scale, True)
        t_ref[...] = jnp.concatenate(pieces, axis=0).T.astype(jnp.bfloat16)

        def step(s, carry):
            slot = near_ref[b, s]
            for m in range(0, size, CHUNK):
                inner = jnp.dot(
                    t_ref[m : m + CHUNK], aug_ref[slot], preferred_element_type=jnp.float32
                )
                prod = jnp.exp2(inner) * v_ref[slot]
                total = prod[:, 0:128]
                for g in range(1, size // 128):
                    total = total + prod[:, g * 128 : (g + 1) * 128]
                acc_ref[m : m + CHUNK] += total
            return carry

        lax.fori_loop(0, near_count, step, 0, unroll=UNROLL)
        out_ref[b] = acc_ref[...]


def near_apply(near_list, own_t, window_t, values, scale):
    per_device, feat, size = own_t.shape
    window, width = window_t.shape[0], 4 * feat
    vmem = VMEM
    part = pl.pallas_call(
        lambda *refs: near_kernel(scale, *refs),
        out_shape=jax.ShapeDtypeStruct((per_device, size, 128), jnp.float32),
        in_specs=[pl.BlockSpec(memory_space=pltpu.SMEM), vmem, vmem, vmem],
        out_specs=vmem,
        scratch_shapes=[
            pltpu.VMEM((window, width, size), jnp.bfloat16),
            pltpu.VMEM((size, width), jnp.bfloat16),
            pltpu.VMEM((size, 128), jnp.float32),
        ],
        compiler_params=pltpu.CompilerParams(vmem_limit_bytes=48 * 1024 * 1024),
        name="near",
    )(near_list, own_t, window_t, values)
    return jnp.sum(part, axis=-1)


def gaussian(inner_prod, target_sq, source_sq, feat_count):
    return jnp.exp(-(target_sq + source_sq - 2.0 * inner_prod) / feat_count)


def shards(
    points,
    leaf_maps,
    root_maps,
    current,
    krylov_basis,
    ritz_roots,
    point_order,
    skeleton,
    root_skeleton,
    near_list,
    far_list,
):
    per_device, skel_count, leaf_size = leaf_maps.shape
    feat_count = points.shape[1]
    sub_count = lax.axis_size("sub")
    sub_leaves = per_device * sub_count
    leaf_count = lax.axis_size("leaf")
    leaf_index = lax.axis_index("leaf")
    own_points = points.reshape(per_device, leaf_size, feat_count)
    own_t = own_points.transpose(0, 2, 1)
    window_t = gather_window(own_t, 1).reshape(3 * sub_leaves, feat_count, leaf_size)
    scale = 1.4426950408889634 / feat_count

    def pick(points_t, index):
        chosen = index[..., None, :] == jnp.arange(leaf_size, dtype=jnp.int32)[:, None]
        return jnp.einsum(
            "...fn,...nk->...kf", points_t, chosen.astype(jnp.float32), precision=HIGHEST_PREC
        )

    lanes = 128
    rows = sub_leaves * leaf_size // lanes
    in_row = point_order[:, None] // lanes == jnp.arange(rows, dtype=jnp.int32)[None, :]
    in_lane = point_order[:, None] % lanes == jnp.arange(lanes, dtype=jnp.int32)[None, :]
    in_row, in_lane = in_row.astype(jnp.float32), in_lane.astype(jnp.float32)
    own_rows = per_device * leaf_size // lanes
    user_subtree, slot_index = exchange(
        [
            Channel(current.reshape(own_rows, lanes), (sub_count,), sub_peers(), sub_slot),
            Channel(
                skeleton.astype(jnp.float32), (3 * sub_count,), window_peers(), window_slot
            ),
        ],
        2,
    )
    window_skel = slot_index.reshape(3 * sub_leaves, skel_count).astype(jnp.int32)
    picked = jnp.dot(in_row, user_subtree.reshape(rows, lanes), precision=HIGHEST_PREC)
    tree_vector = jnp.sum(picked * in_lane, axis=1)

    skel_points = pick(own_t, skeleton)
    skel_sq = jnp.sum(skel_points * skel_points, axis=-1)
    far_points = pick(window_t[far_list], window_skel[far_list])
    far_inner = jnp.einsum("bmf,bjnf->bjmn", skel_points, far_points, precision=HIGHEST_PREC)
    far_kernel = gaussian(
        far_inner,
        skel_sq[:, None, :, None],
        jnp.sum(far_points * far_points, axis=-1)[:, :, None, :],
        feat_count,
    )
    subtree_points = window_t[sub_leaves : 2 * sub_leaves]
    root_index = root_skeleton[0]
    own_root = subtree_points[root_index // leaf_size, :, root_index % leaf_size]
    distance = (jnp.arange(leaf_count, dtype=jnp.int32) - leaf_index) % leaf_count
    far_mask = (distance >= 1).astype(jnp.float32)

    def make_top(all_roots_t):
        all_roots = all_roots_t.transpose(0, 2, 1).reshape(leaf_count * skel_count, feat_count)
        own_root_sq = jnp.sum(own_root * own_root, axis=-1)
        all_root_sq = jnp.sum(all_roots * all_roots, axis=-1)
        top_inner = jnp.dot(own_root, all_roots.T, precision=HIGHEST_PREC)
        kernel = gaussian(top_inner, own_root_sq[:, None], all_root_sq[None, :], feat_count)
        return kernel * jnp.repeat(far_mask, skel_count)[None, :]

    def operator(vector, top_kernel=None):
        values = vector.reshape(per_device, leaf_size)
        skel_weights = jnp.einsum("bkn,bn->bk", leaf_maps, values, precision=HIGHEST_PREC)
        root_part = jnp.einsum("bkn,bn->k", root_maps, values, precision=HIGHEST_PREC)
        packed = jnp.concatenate([values, skel_weights], axis=1)
        channels = [
            Channel(packed, (3 * sub_count,), window_peers(), window_slot),
            Channel(root_part[None], (leaf_count * sub_count,), all_peers(), all_slot),
        ]
        if top_kernel is None:
            channels.append(Channel(own_root.T, (leaf_count,), leaf_peers(), leaf_slot))
            window_values, root_parts, all_roots_t = exchange(channels, 3)
            top_kernel = make_top(all_roots_t)
        else:
            window_values, root_parts = exchange(channels, 4)
        window_values = window_values.reshape(3 * sub_leaves, leaf_size + skel_count)
        root_weights = jnp.sum(root_parts.reshape(leaf_count, sub_count, skel_count), axis=1)
        window_entries = window_values[:, :leaf_size]

        result = near_apply(near_list, own_t, window_t, window_entries[:, None, :], scale)
        skel_out = jnp.einsum(
            "bjmn,bjn->bm",
            far_kernel,
            window_values[far_list][:, :, leaf_size:],
            precision=HIGHEST_PREC,
        )
        result = result + jnp.einsum("bkn,bk->bn", leaf_maps, skel_out, precision=HIGHEST_PREC)
        root_out = jnp.dot(top_kernel, root_weights.reshape(-1), precision=HIGHEST_PREC)
        result = result + jnp.einsum("bkn,k->bn", root_maps, root_out, precision=HIGHEST_PREC)
        return result.reshape(-1) + RIDGE_SHIFT * vector, top_kernel

    applied, top_kernel = operator(tree_vector)
    first_section = tree_vector - applied / ritz_roots[0]
    applied, top_kernel = operator(first_section, top_kernel)
    second = first_section - applied / ritz_roots[1]
    preconditioned = tree_vector - second
    placed = jnp.einsum(
        "ir,il->rl", in_row, preconditioned[:, None] * in_lane, precision=HIGHEST_PREC
    ).reshape(sub_count, own_rows, lanes)
    (pieces,) = exchange([Channel(placed, (sub_count,), sub_peers(), sub_slot, True)], 5)
    user_grown = jnp.sum(pieces, axis=0).reshape(-1)
    local_proj = jnp.dot(krylov_basis, user_grown, precision=HIGHEST_PREC)
    local_gram = jnp.dot(krylov_basis, krylov_basis.T, precision=HIGHEST_PREC)
    basis_count = local_proj.shape[0]
    square = jnp.sum(user_grown * user_grown)
    totals = jnp.concatenate([local_proj, square[None], local_gram.reshape(-1)])
    width = -(-totals.shape[0] // lanes) * lanes
    totals = jnp.pad(totals, (0, width - totals.shape[0]))
    (every,) = exchange(
        [Channel(totals[None], (leaf_count * sub_count,), all_peers(), all_slot)], 6
    )
    totals = jnp.sum(every, axis=(0, 1))
    projections, squares = totals[:basis_count], totals[basis_count]
    gram_matrix = totals[basis_count + 1 : basis_count + 1 + basis_count * basis_count]
    gram_matrix = gram_matrix.reshape(basis_count, basis_count)
    orthogonal = user_grown - jnp.dot(projections, krylov_basis, precision=HIGHEST_PREC)
    length_sq = (
        squares
        - 2.0 * jnp.dot(projections, projections, precision=HIGHEST_PREC)
        + jnp.dot(
            projections,
            jnp.dot(gram_matrix, projections, precision=HIGHEST_PREC),
            precision=HIGHEST_PREC,
        )
    )
    length_norm = jnp.sqrt(length_sq + EPSILON)
    return (orthogonal, jnp.concatenate([projections, length_norm[None]]))


def solution(mesh):
    return jax.shard_map(
        shards,
        mesh=mesh,
        in_specs=(
            P(("leaf", "sub"), None),
            P(("leaf", "sub"), None, None),
            P(("leaf", "sub"), None, None),
            P(("leaf", "sub")),
            P(None, ("leaf", "sub")),
            P(),
            P(("leaf", "sub")),
            P(("leaf", "sub"), None),
            P("leaf", None),
            P(("leaf", "sub"), None),
            P(("leaf", "sub"), None),
        ),
        out_specs=(P(("leaf", "sub")), P()),
        check_vma=False,
    )
```
